32 devices in a mesh: center: 8 (over z, y), rep: 4 (over x, core).
Axes of the slice: x: 2, y: 2, z: 4, core: 2. Of those that a mesh axis runs over, the one named last changes fastest.
Arguments:
- faces: bfloat16 [2048, 512], P(('center', 'rep')), may hold values from -1800 to 1800
- w_first: bfloat16 [512, 512], replicated, may hold values from -1.1 to 1.1
- w_second: bfloat16 [512, 512], replicated, may hold values from -1.1 to 1.1
- gain_first: float32 [512], replicated, may hold values from 0.46 to 1.54
- bias_first: float32 [512], replicated, may hold values from -3 to 3
- gain_second: float32 [512], replicated, may hold values from 0.46 to 1.54
- centers: float32 [16384, 512], P('center'), may hold values from -6 to 6
- momentum: float32 [16384, 512], P('center'), may hold values from -1.2 to 1.2
- sample_index: int32 [1024], P('center'), may hold values from 0 to 2047, as said below
- live_count: int32 [8], P('center'), may hold values from 16 to 128, as said below
- labels: int32 [2048], P(('center', 'rep')), may hold values from 0 to 1023, as said below
Outputs:
- loss: float32 [2048], P(('center', 'rep'))
- feat_grad: float32 [2048, 512], P(('center', 'rep'))
- new_centers: float32 [1024, 512], P('center')
- new_momentum: float32 [1024, 512], P('center')
The draws below stay inside these ranges and needn't reach their ends.
Inputs may be any that keep to these rules, and one draw needn't show every extreme that they name: `sample_index`: the 128 entries of one shard are distinct rows of that shard. The live slots of a shard are its first live_count entries; some shard has 128 of them and some shard 128 // 8. `labels`: each label is a live sampled slot, counted over all shards' lists in shard order.
All inputs are finite; a program needn't handle non-finite values.
Results may differ from the reference program's by a relative error of at most 0.0075.
Values may be sent and summed in bfloat16 or wider, within the bound.
No kernel may reach another device: no remote copies, remote signals or barrier semaphores. Data moves between devices by JAX's collectives and lax.ppermute only.
A program may use at most 64 MiB of HBM per device.

```python
import math
import jax
import jax.numpy as jnp
from jax import lax

D = 512
FACE_DEV = 64
ROWS_DEV = 2048
SAMP = 128
SHARDS = 8
REPS = 4
FACES = 2048
CENTERS = 16384
SAMPLED = 1024


def head_params(key):
    subkeys = jax.random.split(jax.random.fold_in(key, 3), 5)
    scale_in = 1.0 / math.sqrt(D)
    w_first = jnp.clip(jax.random.normal(subkeys[0], (D, D), jnp.float32), -6.0, 6.0) * scale_in
    w_second = jnp.clip(jax.random.normal(subkeys[1], (D, D), jnp.float32), -6.0, 6.0) * scale_in
    gain_first = 1.0 + 0.18 * jnp.clip(jax.random.normal(subkeys[2], (D,), jnp.float32), -3.0, 3.0)
    bias_first = 0.5 * jnp.clip(jax.random.normal(subkeys[3], (D,), jnp.float32), -6.0, 6.0)
    gain_second = 1.0 + 0.18 * jnp.clip(jax.random.normal(subkeys[4], (D,), jnp.float32), -3.0, 3.0)
    return (w_first, w_second, gain_first, bias_first, gain_second)


def draw_w_first(key, part):
    return head_params(key)[0].astype(jnp.bfloat16)


def draw_w_second(key, part):
    return head_params(key)[1].astype(jnp.bfloat16)


def draw_gain_first(key, part):
    return head_params(key)[2]


def draw_bias_first(key, part):
    return head_params(key)[3]


def draw_gain_second(key, part):
    return head_params(key)[4]


def draw_sample_index(key, part):
    shard_keys = jax.random.split(jax.random.fold_in(key, 11), SHARDS)

    def one_shard(shard_key):
        return jax.random.permutation(shard_key, ROWS_DEV)[:SAMP]
    chosen = jax.vmap(one_shard)(shard_keys)
    return chosen.reshape(SHARDS * SAMP).astype(jnp.int32)


def live_and_labels(key):
    base_key = jax.random.fold_in(key, 7)
    key_count, key_full, key_low, key_owner, key_slot = jax.random.split(base_key, 5)
    counts = jax.random.randint(key_count, (SHARDS,), SAMP // 8, SAMP + 1)
    full_shard = jax.random.randint(key_full, (), 0, SHARDS)
    low_shard = (full_shard + 1 + jax.random.randint(key_low, (), 0, SHARDS - 1)) % SHARDS
    counts = counts.at[low_shard].set(SAMP // 8).at[full_shard].set(SAMP)
    owners = jax.random.randint(key_owner, (FACES,), 0, SHARDS)
    slot_draw = jax.random.randint(key_slot, (FACES,), 0, 1 << 20) % counts[owners]
    label_vals = owners * SAMP + slot_draw
    return (counts.astype(jnp.int32), label_vals.astype(jnp.int32))


def draw_live_count(key, part):
    return live_and_labels(key)[0]


def draw_labels(key, part):
    return live_and_labels(key)[1]


def face_values(key):
    key_rows, key_cols, key_base = jax.random.split(key, 3)
    block_ids = jnp.arange(FACES) // FACE_DEV
    rising = 1.0 + 2.0 * (block_ids % REPS).astype(jnp.float32) / max(REPS - 1, 1)
    col_scale = jnp.exp(jax.random.uniform(key_cols, (1, D), jnp.float32, 0.0, math.log(10.0)))
    row_scale = jnp.exp(jax.random.uniform(key_rows, (FACES, 1), jnp.float32, 0.0, math.log(10.0)))
    base_vals = jnp.clip(jax.random.normal(key_base, (FACES, D), jnp.float32), -6.0, 6.0)
    return base_vals * row_scale * col_scale * rising[:, None]


def draw_faces(key, part):
    return face_values(key).astype(jnp.bfloat16)


def draw_centers(key, part):
    key_noise = jax.random.fold_in(jax.random.fold_in(key, 17), 1)
    noise = jnp.clip(jax.random.normal(key_noise, (CENTERS, D), jnp.float32), -6.0, 6.0)
    values = noise
    return jnp.clip(values, -6.0, 6.0)


def steps_of(own_key, dims, cuts, smallest, top_value):
    loudness = 1.0
    for axis_at, parts in cuts:
        draws = jax.random.uniform(jax.random.fold_in(jax.random.fold_in(own_key, 6), axis_at), (parts,), jnp.float32, smallest / len(cuts), top_value / len(cuts))
        loudness = loudness * jnp.repeat(jnp.exp(draws), dims[axis_at] // parts).reshape((-1,) + (1,) * (len(dims) - 1 - axis_at))
    return loudness


def gaussian(stream_key, dims, scale, bound, cuts=(), held_as=jnp.bfloat16):
    array = jax.random.normal(stream_key, dims, jnp.float32) * scale
    if len(cuts) > 0:
        array = steps_of(stream_key, dims, cuts, -0.22, 0.18) * array
    return jnp.clip(array, min=-bound, max=bound).astype(held_as)


def setup_inputs(seed: int = 0) -> dict:
    splits = jax.random.split(jax.random.key(seed), 12)
    faces = draw_faces(jax.random.fold_in(splits[11], 71), 0)
    w_first = draw_w_first(jax.random.fold_in(splits[11], 71), 0)
    w_second = draw_w_second(jax.random.fold_in(splits[11], 71), 0)
    gain_first = draw_gain_first(jax.random.fold_in(splits[11], 71), 0)
    bias_first = draw_bias_first(jax.random.fold_in(splits[11], 71), 0)
    gain_second = draw_gain_second(jax.random.fold_in(splits[11], 71), 0)
    centers = draw_centers(jax.random.fold_in(splits[11], 71), 0)
    momentum = gaussian(splits[7], (CENTERS, D), 0.2, 1.2, ((0, 8),), jnp.float32)
    sample_index = draw_sample_index(jax.random.fold_in(splits[11], 71), 0)
    live_count = draw_live_count(jax.random.fold_in(splits[11], 71), 0)
    labels = draw_labels(jax.random.fold_in(splits[11], 71), 0)
    return dict(faces=faces, w_first=w_first, w_second=w_second, gain_first=gain_first, bias_first=bias_first, gain_second=gain_second, centers=centers, momentum=momentum, sample_index=sample_index, live_count=live_count, labels=labels)


LOGIT_SCALE = 64.0
COS_MARGIN = 0.35
LEARN_RATE = 0.5
MOMENT_COEF = 0.9
DECAY_COEF = 0.0005
NORM_EPS = 1e-05
LENGTH_EPS = 1e-06

def normalize_batch(values, gain_vec):
    grouped = values.reshape(-1, FACE_DEV * REPS, values.shape[1])
    mean_vec = lax.optimization_barrier(jnp.mean(grouped, 1, keepdims=True))
    centered = grouped - mean_vec
    spread = lax.optimization_barrier(jnp.mean(centered * centered, 1, keepdims=True))
    return (gain_vec * centered * lax.rsqrt(spread + NORM_EPS)).reshape(values.shape)

def reference(faces, w_first, w_second, gain_first, bias_first, gain_second, centers, momentum, sample_index, live_count, labels):
    first_out = jnp.dot(faces, w_first, preferred_element_type=jnp.float32)
    hidden = jnp.maximum(normalize_batch(first_out, gain_first) + bias_first, 0.0).astype(jnp.bfloat16)
    second = jnp.dot(hidden, w_second, preferred_element_type=jnp.float32)
    feature = normalize_batch(second, gain_second)
    length = jnp.sqrt(lax.optimization_barrier(jnp.sum(feature * feature, 1, keepdims=True)) + LENGTH_EPS)
    unit_rows = feature / length
    unit_low = unit_rows.astype(jnp.bfloat16)
    slot_ids = jnp.arange(SAMPLED).astype(jnp.int32)
    owner = (slot_ids // SAMP).astype(jnp.int32)
    table_rows = (owner * ROWS_DEV + sample_index).astype(jnp.int32)
    picked = jnp.take(centers, table_rows, axis=0)
    picked_momentum = jnp.take(momentum, table_rows, axis=0)
    center_len = jnp.sqrt(lax.optimization_barrier(jnp.sum(picked * picked, 1, keepdims=True)) + LENGTH_EPS)
    center_unit = picked / center_len
    center_low = center_unit.astype(jnp.bfloat16)
    live_slot = slot_ids % SAMP < jnp.take(live_count, owner)
    block_rows = min(1024, FACES)
    unit_blocks = unit_low.reshape(FACES // block_rows, block_rows, D)
    label_blocks = labels.reshape(FACES // block_rows, block_rows)

    def score_block(running, element):
        unit_block, mark_block = element
        cosine = jnp.dot(unit_block, center_low.T, preferred_element_type=jnp.float32)
        target = mark_block[:, None] == slot_ids[None, :]
        logits = LOGIT_SCALE * (cosine - COS_MARGIN * target.astype(jnp.float32))
        exponent = jnp.where(live_slot[None, :], jnp.exp(logits), 0.0)
        softmax_total = lax.optimization_barrier(jnp.sum(exponent, 1))
        target_logit = lax.optimization_barrier(jnp.sum(jnp.where(target, logits, 0.0), 1))
        face_loss = jnp.log(softmax_total) - target_logit
        weight = (LOGIT_SCALE * (exponent / softmax_total[:, None] - target.astype(jnp.float32))).astype(jnp.bfloat16)
        unit_grad = jnp.dot(weight, center_low, preferred_element_type=jnp.float32)
        running = running + jnp.dot(weight.T, unit_block, preferred_element_type=jnp.float32)
        return (running, (face_loss, unit_grad))
    start_sum = jnp.zeros((SAMPLED, D), jnp.float32)
    center_raw, (loss_blocks, grad_blocks) = lax.scan(score_block, start_sum, (unit_blocks, label_blocks))
    loss = loss_blocks.reshape(FACES)
    unit_grad = grad_blocks.reshape(FACES, D)
    radial = lax.optimization_barrier(jnp.sum(unit_rows * unit_grad, 1, keepdims=True))
    feat_grad = (unit_grad - unit_rows * radial) / length
    center_radial = lax.optimization_barrier(jnp.sum(center_unit * center_raw, 1, keepdims=True))
    center_grad = (center_raw - center_unit * center_radial) / center_len
    velocity = MOMENT_COEF * picked_momentum + center_grad + DECAY_COEF * picked
    new_momentum = jnp.where(live_slot[:, None], velocity, picked_momentum)
    new_centers = jnp.where(live_slot[:, None], picked - LEARN_RATE * new_momentum, picked)
    return (loss, feat_grad, new_centers, new_momentum)
```

```python
import functools

import jax
import jax.numpy as jnp
from jax import lax
from jax.experimental import pallas as pl
from jax.experimental.pallas import tpu as pltpu
from jax.sharding import PartitionSpec as P


LOGIT_SCALE = 64.0
COS_MARGIN = 0.35
LEARN_RATE = 0.5
MOMENT_COEF = 0.9
DECAY_COEF = 0.0005
NORM_EPS = 1e-05
LENGTH_EPS = 1e-06
DEAD_MARK = 2.0
LABEL_BASE = 128
LABEL_ROWS = 16

F32 = jnp.float32
BF16 = jnp.bfloat16
VMEM = pl.BlockSpec(memory_space=pltpu.VMEM)
HBM = pl.BlockSpec(memory_space=pltpu.HBM)
SMEM = pl.BlockSpec(memory_space=pltpu.SMEM)
PARAMS = pltpu.CompilerParams(vmem_limit_bytes=16 * 2**20)


def swap(value, axis, mask):
    size = lax.axis_size(axis)
    return lax.ppermute(value, axis, [(i, i ^ mask) for i in range(size)])


def rep_bits():
    bit = lax.axis_size("rep") >> 1
    while bit:
        yield bit
        bit >>= 1


def stages_of(size):
    bits = size.bit_length() - 1
    stages, low = [], 0
    while low < bits:
        take = 1 if low == 0 else min(2, bits - low)
        stages.append([step << low for step in range(1, 1 << take)])
        low += take
    return stages


def spread_rep(value):
    reps = lax.axis_size("rep")
    masks = [0]
    for bit in rep_bits():
        value = jnp.concatenate([value, swap(value, "rep", bit)], axis=0)
        masks += [mask | bit for mask in masks]
    assert len(masks) == reps
    return value, masks


def entry_kernel(index_ref, live_ref, centers_ref, faces_ref, labels_ref, low_ref, pack_ref, line_ref, index, labels, rows_ref, sems):
    quarter, width = low_ref.shape
    face_rows = faces_ref.shape[0]
    first = lax.axis_index("rep") * quarter
    index_copy = pltpu.make_async_copy(index_ref, index, sems.at[0])
    faces_copy = pltpu.make_async_copy(faces_ref, pack_ref.at[pl.ds(0, face_rows)], sems.at[2])
    labels_copy = pltpu.make_async_copy(labels_ref, labels, sems.at[3])
    index_copy.start()
    labels_copy.start()
    faces_copy.start()
    index_copy.wait()
    for i in range(quarter):
        row = index[first + i]
        pltpu.make_async_copy(centers_ref.at[pl.ds(row, 1)], rows_ref.at[pl.ds(i, 1)], sems.at[4]).start()
    labels_copy.wait()
    marks = jnp.concatenate([labels[...]] * (width // face_rows), axis=1)
    line = lax.broadcasted_iota(jnp.int32, (LABEL_ROWS, width), 0)
    digits = jnp.where(line == 0, marks // LABEL_BASE, jnp.where(line == 1, marks % LABEL_BASE, 0))
    pack_ref[face_rows:] = digits.astype(F32).astype(BF16)
    line_ref[...] = jnp.full(line_ref.shape, live_ref[0], jnp.int32)
    faces_copy.wait()
    pltpu.make_async_copy(rows_ref, rows_ref, sems.at[4]).wait()
    picked = rows_ref[...]
    unit = picked / jnp.sqrt(jnp.sum(picked * picked, 1, keepdims=True) + LENGTH_EPS)
    slot = lax.broadcasted_iota(jnp.int32, (quarter, width), 0) + first
    low_ref[...] = jnp.where(slot < live_ref[0], unit, DEAD_MARK).astype(BF16)


def rows_kernel(index_ref, centers_ref, momentum_ref, after_ref, picked_ref, moment_ref, index, sems):
    del after_ref
    index_copy = pltpu.make_async_copy(index_ref, index, sems.at[2])
    index_copy.start()
    index_copy.wait()
    for i in range(index.shape[0]):
        row = index[i]
        pltpu.make_async_copy(centers_ref.at[pl.ds(row, 1)], picked_ref.at[pl.ds(i, 1)], sems.at[0]).start()
        pltpu.make_async_copy(momentum_ref.at[pl.ds(row, 1)], moment_ref.at[pl.ds(i, 1)], sems.at[1]).start()
    pltpu.make_async_copy(picked_ref, picked_ref, sems.at[0]).wait()
    pltpu.make_async_copy(moment_ref, moment_ref, sems.at[1]).wait()


def normalized(values, gain):
    count = values.shape[0]
    centered = values - jnp.sum(values, 0, keepdims=True) / count
    spread = jnp.sum(centered * centered, 0, keepdims=True) / count
    return centered * (gain * lax.rsqrt(spread + NORM_EPS))


def head_kernel(
    w_first_ref, w_second_ref, gain_first_ref, bias_first_ref, gain_second_ref, packs_ref, low_ref, feature_ref, label_ref, w_first, w_second, sems
):
    first_copy = pltpu.make_async_copy(w_first_ref, w_first, sems.at[0])
    second_copy = pltpu.make_async_copy(w_second_ref, w_second, sems.at[1])
    first_copy.start()
    second_copy.start()
    face_rows = feature_ref.shape[0]
    each = face_rows + LABEL_ROWS
    packs = [packs_ref[at * each : (at + 1) * each] for at in range(packs_ref.shape[0] // each)]
    faces = jnp.concatenate([pack[:face_rows] for pack in packs], axis=0)
    group = label_ref.shape[1]
    part = lax.broadcasted_iota(jnp.int32, (LABEL_ROWS, group), 1) // face_rows
    digits = packs[0][face_rows:, :group].astype(F32)
    for at, pack in enumerate(packs[1:], 1):
        digits = jnp.where(part == at, pack[face_rows:, :group].astype(F32), digits)
    label_ref[...] = jnp.broadcast_to(digits[0:1] * LABEL_BASE + digits[1:2], label_ref.shape).astype(jnp.int32)
    first_copy.wait()
    first = jnp.dot(faces, w_first[...], preferred_element_type=F32)
    hidden = jnp.maximum(normalized(first, gain_first_ref[...]) + bias_first_ref[...], 0.0).astype(BF16)
    second_copy.wait()
    second = jnp.dot(hidden, w_second[...], preferred_element_type=F32)
    feature = normalized(second, gain_second_ref[...])
    length = jnp.sqrt(jnp.sum(feature * feature, 1, keepdims=True) + LENGTH_EPS)
    low_ref[...] = (feature / length).astype(BF16)
    feature_ref[...] = feature[:face_rows]


def target_of(label_ref, slots, quarter, slot_count):
    at = lax.broadcasted_iota(jnp.int32, (slots, label_ref.shape[1]), 0)
    shard = lax.axis_index("center") ^ (at // quarter)
    slot = shard * slot_count + lax.axis_index("rep") * quarter + at % quarter
    return slot == label_ref[0:1]


def score_kernel(quarter, slot_count, unit_ref, label_ref, *refs):
    blocks, (exponent_ref, sums_ref) = refs[:-2], refs[-2:]
    rows = jnp.concatenate([block[...] for block in blocks], axis=0)
    cosine = lax.dot_general(rows, unit_ref[...], (((1,), (1,)), ((), ())), preferred_element_type=F32)
    target = target_of(label_ref, rows.shape[0], quarter, slot_count)
    logits = LOGIT_SCALE * (cosine - jnp.where(target, COS_MARGIN, 0.0))
    live = rows[:, 0:1].astype(F32) < DEAD_MARK
    exponent = jnp.where(live, jnp.exp(logits), 0.0)
    exponent_ref[...] = exponent
    total = jnp.sum(exponent, 0, keepdims=True)
    own = jnp.sum(jnp.where(target, logits, 0.0), 0, keepdims=True)
    line = lax.broadcasted_iota(jnp.int32, sums_ref.shape, 0)
    sums_ref[...] = jnp.where(line == 0, total, own)


def fold_lanes(sums, bit, face_rows):
    count = sums.shape[1] // face_rows
    parts = [sums[:, (at ^ bit) * face_rows : ((at ^ bit) + 1) * face_rows] for at in range(count)]
    return jnp.concatenate(parts, axis=1)


def total_kernel(bit, face_rows, own_ref, other_ref, out_ref):
    out_ref[...] = own_ref[...] + fold_lanes(other_ref[...], bit, face_rows)


def grad_kernel(quarter, slot_count, unit_ref, label_ref, exponent_ref, own_ref, other_ref, *refs):
    blocks, (loss_ref, kept_ref, face_ref, even_ref, odd_ref) = refs[:-5], refs[-5:]
    group = unit_ref.shape[0]
    face_rows = loss_ref.shape[1]
    summed = own_ref[...] + fold_lanes(other_ref[...], 1, face_rows)
    total = summed[0:1]
    loss_ref[...] = (jnp.log(total) - summed[1:2])[:, :face_rows]
    rows = jnp.concatenate([block[...] for block in blocks], axis=0)
    target = target_of(label_ref, rows.shape[0], quarter, slot_count)
    share = exponent_ref[...] / total
    weight = (LOGIT_SCALE * (share - jnp.where(target, 1.0, 0.0))).astype(BF16)
    raw = jnp.dot(weight, unit_ref[...], preferred_element_type=F32)
    for at in range(rows.shape[0] // quarter):
        half = odd_ref if at % 2 else even_ref
        half[pl.ds(at // 2 * quarter, quarter)] = raw[at * quarter : (at + 1) * quarter].astype(half.dtype)
    unit_grad = lax.dot_general(weight, rows, (((0,), (0,)), ((), ())), preferred_element_type=F32)
    kept_ref[...] = unit_grad[: group // 2]
    face_ref[...] = unit_grad[group // 2 :].astype(BF16)


def fold_kernel(parts, kept_ref, *refs):
    takes, (own_ref, *outs) = refs[:parts], refs[parts:]
    summed = kept_ref[...]
    for item in takes:
        summed = summed + item[...].astype(F32)
    rows = own_ref.shape[0]
    own_ref[...] = summed[:rows].astype(own_ref.dtype)
    for at, out in enumerate(outs, 1):
        out[...] = summed[at * rows : (at + 1) * rows].astype(BF16)


def half_kernel(kept_ref, received_ref, own_ref, sent_ref):
    rows = own_ref.shape[0]
    summed = kept_ref[...] + received_ref[...].astype(F32)
    own_ref[...] = summed[:rows]
    sent_ref[...] = summed[rows:].astype(BF16)


def face_kernel(feature_ref, own_ref, received_ref, grad_ref):
    feature = feature_ref[...]
    length = jnp.sqrt(jnp.sum(feature * feature, 1, keepdims=True) + LENGTH_EPS)
    unit = feature / length
    unit_grad = own_ref[...] + received_ref[...].astype(F32)
    radial = jnp.sum(unit * unit_grad, 1, keepdims=True)
    grad_ref[...] = (unit_grad - unit * radial) / length


def step_kernel(masks, live_ref, picked_ref, moment_ref, raws_ref, placed_ref, velocity_ref, raw_ref):
    quarter = raws_ref.shape[0] // len(masks)
    rep = lax.axis_index("rep")
    for at, mask in enumerate(masks):
        item = raws_ref[at * quarter : (at + 1) * quarter].astype(F32)
        raw_ref[pl.ds(pl.multiple_of((rep ^ mask) * quarter, quarter), quarter)] = item
    raw = raw_ref[...]
    picked = picked_ref[...]
    moment = moment_ref[...]
    length = jnp.sqrt(jnp.sum(picked * picked, 1, keepdims=True) + LENGTH_EPS)
    unit = picked / length
    radial = jnp.sum(unit * raw, 1, keepdims=True)
    grad = (raw - unit * radial) / length
    live = lax.broadcasted_iota(jnp.int32, picked.shape, 0) < live_ref[0:1, 0:1]
    velocity = jnp.where(live, MOMENT_COEF * moment + grad + DECAY_COEF * picked, moment)
    velocity_ref[...] = velocity
    placed_ref[...] = jnp.where(live, picked - LEARN_RATE * velocity, picked)


def per_device(
    faces,
    w_first,
    w_second,
    gain_first,
    bias_first,
    gain_second,
    centers,
    momentum,
    sample_index,
    live_count,
    labels,
):
    face_rows, width = faces.shape
    faces, w_first, w_second, centers, momentum, sample_index, labels = (
        pltpu.with_memory_space_constraint(value, pltpu.HBM)
        for value in (faces, w_first, w_second, centers, momentum, sample_index, labels.reshape(1, face_rows))
    )
    reps = lax.axis_size("rep")
    shards = lax.axis_size("center")
    slot_count = sample_index.shape[0]
    quarter = slot_count // reps
    group = face_rows * reps
    slots = quarter * shards
    shape = jax.ShapeDtypeStruct

    low, pack, live_line = pl.pallas_call(
        entry_kernel,
        in_specs=[HBM, SMEM, HBM, HBM, HBM],
        out_specs=[VMEM] * 3,
        out_shape=[
            shape((quarter, width), BF16),
            shape((face_rows + LABEL_ROWS, width), BF16),
            shape((8, 128), jnp.int32),
        ],
        scratch_shapes=[
            pltpu.SMEM((slot_count,), jnp.int32),
            pltpu.VMEM((1, face_rows), jnp.int32),
            pltpu.VMEM((quarter, width), F32),
            pltpu.SemaphoreType.DMA((5,)),
        ],
        compiler_params=PARAMS,
        name="entry",
    )(sample_index, live_count, centers, faces, labels)

    blocks = [low]
    stages = stages_of(shards)
    for masks in stages:
        joined = jnp.concatenate(blocks, axis=0) if len(blocks) > 1 else blocks[0]
        blocks = [joined] + [swap(joined, "center", mask) for mask in masks]

    packs, masks = spread_rep(pack)
    order = [masks.index(at) for at in range(reps)]
    each = face_rows + LABEL_ROWS
    if order != list(range(reps)):
        packs = jnp.concatenate([packs[at * each : (at + 1) * each] for at in order], axis=0)
    unit_low, feature, label_line = pl.pallas_call(
        head_kernel,
        in_specs=[HBM] * 2 + [VMEM] * 4,
        out_specs=[VMEM] * 3,
        out_shape=[shape((group, width), BF16), shape((face_rows, width), F32), shape((8, group), jnp.int32)],
        scratch_shapes=[pltpu.VMEM((width, width), BF16)] * 2 + [pltpu.SemaphoreType.DMA((2,))],
        compiler_params=PARAMS,
        name="head",
    )(w_first, w_second, gain_first.reshape(1, width), bias_first.reshape(1, width), gain_second.reshape(1, width), packs)

    exponent, sums = pl.pallas_call(
        functools.partial(score_kernel, quarter, slot_count),
        in_specs=[VMEM] * (2 + len(blocks)),
        out_specs=[VMEM] * 2,
        out_shape=[shape((slots, group), F32), shape((8, group), F32)],
        compiler_params=PARAMS,
        name="score",
    )(unit_low, label_line, *blocks)

    bits = list(rep_bits())
    for bit in bits[:-1]:
        sums = pl.pallas_call(
            functools.partial(total_kernel, bit, face_rows),
            in_specs=[VMEM] * 2,
            out_specs=VMEM,
            out_shape=shape((8, group), F32),
            compiler_params=PARAMS,
            name="total",
        )(sums, swap(sums, "rep", bit))
    loss, face_kept, face_sent, kept, sent = pl.pallas_call(
        functools.partial(grad_kernel, quarter, slot_count),
        in_specs=[VMEM] * (5 + len(blocks)),
        out_specs=[VMEM] * 5,
        out_shape=[
            shape((1, face_rows), F32),
            shape((group // 2, width), F32),
            shape((group // 2, width), BF16),
            shape((slots // 2, width), F32),
            shape((slots // 2, width), BF16),
        ],
        compiler_params=PARAMS,
        name="grad",
    )(unit_low, label_line, exponent, sums, swap(sums, "rep", 1), *blocks)

    picked, moment = pl.pallas_call(
        rows_kernel,
        in_specs=[HBM] * 3 + [VMEM],
        out_specs=[VMEM, VMEM],
        out_shape=[shape((slot_count, width), F32)] * 2,
        scratch_shapes=[pltpu.SMEM((slot_count,), jnp.int32), pltpu.SemaphoreType.DMA((3,))],
        compiler_params=PARAMS,
        name="rows",
    )(sample_index, centers, momentum, loss)

    received = [swap(sent, "center", 1)]
    for later in stages[:0:-1] + [[]]:
        rows = kept.shape[0] // (len(later) + 1)
        kept, *sends = pl.pallas_call(
            functools.partial(fold_kernel, len(received)),
            in_specs=[VMEM] * (1 + len(received)),
            out_specs=[VMEM] * (1 + len(later)),
            out_shape=[shape((rows, width), F32 if later else BF16)] + [shape((rows, width), BF16)] * len(later),
            compiler_params=PARAMS,
            name="fold",
        )(kept, *received)
        received = [swap(item, "center", mask) for mask, item in zip(later, sends)]

    for bit in bits[:-1]:
        half = face_kept.shape[0] // 2
        face_kept, face_sent = pl.pallas_call(
            half_kernel,
            in_specs=[VMEM] * 2,
            out_specs=[VMEM] * 2,
            out_shape=[shape((half, width), F32), shape((half, width), BF16)],
            compiler_params=PARAMS,
            name="half",
        )(face_kept, swap(face_sent, "rep", bit))
    feat_grad = pl.pallas_call(
        face_kernel,
        in_specs=[VMEM] * 3,
        out_specs=VMEM,
        out_shape=shape((face_rows, width), F32),
        compiler_params=PARAMS,
        name="face",
    )(feature, face_kept, swap(face_sent, "rep", bits[-1]))

    raws, masks = spread_rep(kept)
    new_centers, new_momentum = pl.pallas_call(
        functools.partial(step_kernel, masks),
        in_specs=[VMEM] * 4,
        out_specs=[VMEM] * 2,
        out_shape=[shape((slot_count, width), F32)] * 2,
        scratch_shapes=[pltpu.VMEM((slot_count, width), F32)],
        compiler_params=PARAMS,
        name="step",
    )(live_line, picked, moment, raws)
    return (loss.reshape(face_rows), feat_grad, new_centers, new_momentum)


def solution(mesh):
    return jax.shard_map(
        per_device,
        mesh=mesh,
        in_specs=(
            P(("center", "rep"), None),
            P(),
            P(),
            P(),
            P(),
            P(),
            P("center", None),
            P("center", None),
            P("center"),
            P("center"),
            P(("center", "rep")),
        ),
        out_specs=(
            P(("center", "rep")),
            P(("center", "rep"), None),
            P("center", None),
            P("center", None),
        ),
        check_vma=False,
    )
```
